32 devices in a mesh: groups: 2 (over x), chol: 16 (over z, y, core).
Axes of the slice: x: 2, y: 2, z: 4, core: 2. Of those that a mesh axis runs over, the one named last changes fastest.
Arguments:
- green_rows: bfloat16 [128, 65536], P('groups', 'chol'), parts along dimension 0, may hold values from -6 to 6
- factors: bfloat16 [5120, 65536], P(None, 'chol'), may hold values from -0.03125 to 0.03125
- noise_draws: float32 [128, 5120], P('groups', 'chol'), parts along dimension 0, may hold values from -6 to 6
Outputs:
- potential: float32 [128, 65536], P('groups', 'chol'), parts along dimension 0
- log_weight: float32 [128], P(('groups', 'chol')), parts along dimension 0
The draws below stay inside these ranges and needn't reach their ends.
There are 2 independent parts, one for each index of `groups`. The reference program is written for one: setup_inputs(seed, part) draws one part's arguments, and reference() takes and returns one part's arrays. A program takes and returns all parts, laid end to end along the dimension named above; an argument that names none is the same for every part. Nothing has to cross between parts.
All inputs are finite; a program needn't handle non-finite values.
Results may differ from the reference program's by a relative error of at most 0.0029.
Values may be sent and summed in bfloat16 or wider, within the bound.
No kernel may reach another device: no remote copies, remote signals or barrier semaphores. Data moves between devices by JAX's collectives and lax.ppermute only.
A program may use at most 128 MiB of HBM per device.

```python
import math
import jax
import jax.numpy as jnp
from jax import lax

NCHOL = 5120
PAIRS = 65536
WALKERS = 64


def strengthened(array, stream_key, source, target, blocks, factor):
    def block_of(position):
        return (jnp.arange(array.shape[position]) // (array.shape[position] // blocks)).reshape((-1,) + (1,) * (array.ndim - 1 - position))

    one_side = jax.random.permutation(stream_key, blocks)[block_of(target)]
    other_side = (block_of(target) + blocks // 2) % blocks
    return jnp.where((block_of(source) == one_side) | (block_of(source) == other_side), factor * array, array)


def block_scale(key, dims, cuts, smallest, top_value):
    def one(dim, shards_of):
        steps = jax.random.uniform(jax.random.fold_in(jax.random.fold_in(key, 6), dim), (shards_of,), jnp.float32, smallest / len(cuts), top_value / len(cuts))
        return jnp.repeat(jnp.exp(steps), dims[dim] // shards_of).reshape((-1,) + (1,) * (len(dims) - dim - 1))

    loudness = one(*cuts[0])
    for cut in cuts[1:]:
        loudness = loudness * one(*cut)
    return loudness


def gaussian(own_key, dims, scale, most, cuts=(), dtype=jnp.bfloat16):
    entries = scale * jax.random.normal(own_key, dims, jnp.float32)
    if cuts:
        entries = entries * block_scale(own_key, dims, cuts, -0.22, 0.18)
    return jnp.clip(entries, -most, most).astype(dtype)


def noise_with(own_key, shape, spread, bound, pieces, heavy, held_as=jnp.bfloat16):
    result = spread * jax.random.normal(own_key, shape, jnp.float32)
    if pieces:
        result = result * block_scale(own_key, shape, pieces, -0.22, 0.18)
    return jnp.clip(strengthened(result, jax.random.fold_in(own_key, 3), *heavy), -bound, bound).astype(held_as)


def setup_inputs(seed: int = 0, part: int = 0) -> dict:
    key_list = jax.random.split(jax.random.key(seed), 4)
    part_keys = jax.random.split(jax.random.fold_in(key_list[3], part), 4)
    return {
        "green_rows": gaussian(part_keys[0], (WALKERS, PAIRS), 1.0, 6.0, ((1, 16),)),
        "factors": noise_with(key_list[1], (NCHOL, PAIRS), PAIRS ** -0.5, 0.03125, ((1, 16),), (1, 0, 16, 2.0)),
        "noise_draws": gaussian(part_keys[2], (WALKERS, NCHOL), 1.0, 6.0, ((1, 16),), jnp.float32),
    }


def reference(green_rows, factors, noise_draws):
    forces = lax.dot_general(green_rows, factors, (((1,), (1,)), ((), ())), preferred_element_type=jnp.float32)
    capped = jnp.tanh(forces)
    fields = noise_draws - capped
    potential = jnp.dot(fields.astype(jnp.bfloat16), factors, preferred_element_type=jnp.float32)
    log_weight = lax.optimization_barrier(jnp.sum(fields * capped - 0.5 * capped * capped, axis=1)) / math.sqrt(NCHOL)
    return (potential, log_weight)
```

```python
import functools
import math

import jax
import jax.numpy as jnp
from jax import lax
from jax.experimental import pallas as pl
from jax.experimental.pallas import tpu as pltpu
from jax.sharding import PartitionSpec as P

LANES = 128
TILE = 16
MARGIN = 4 * 1024 * 1024
SHARES = 4
BANKS = 4
HELD_BANKS = 4
VMEM = pl.BlockSpec(memory_space=pltpu.VMEM)
HBM = pl.BlockSpec(memory_space=pltpu.HBM)


def pack_rows(rows, pack):
    part = rows.shape[0] // pack
    return jnp.concatenate([rows[i * part : (i + 1) * part] for i in range(pack)], axis=1)


def unpack_rows(rows, pack):
    width = rows.shape[1] // pack
    return jnp.concatenate([rows[:, i * width : (i + 1) * width] for i in range(pack)], axis=0)


def params(limit=MARGIN):
    return pltpu.CompilerParams(vmem_limit_bytes=limit)


def share_of(owner, me):
    return lax.rem(owner, SHARES) ^ lax.rem(me, SHARES)


def forces_kernel(group, pack, rows_hbm, noise_hbm, slabs, kept, sent, draws, *refs):
    *banks, rows_in, noise, sems = refs
    n, size, pairs = slabs.shape
    depth = n // BANKS
    me = lax.axis_index("chol")

    def fetch(d, source, target):
        return pltpu.make_async_copy(source, target, sems.at[d])

    rows_copy = pltpu.make_async_copy(rows_hbm, rows_in, sems.at[n])
    rows_copy.start()
    noise_copy = pltpu.make_async_copy(noise_hbm, noise, sems.at[n + 1])
    noise_copy.start()
    for d in range(n):
        fetch(d, slabs.at[d], banks[d // depth].at[d % depth]).start()
    noise_copy.wait()
    draws[0] = pack_rows(noise[...].T, pack)
    rows_copy.wait()

    def step(source, offset, i, _):
        for j in range(group):
            fetch(i * group + j, slabs.at[i * group + j], source.at[i * group + j - offset]).wait()
        block = source[pl.ds(i * group - offset, group)].reshape(group * size, pairs)
        part = lax.dot_general(
            block, rows_in[...], (((1,), (1,)), ((), ())), preferred_element_type=jnp.float32
        )
        for j in range(group):
            owner = i * group + j
            share = share_of(owner, me)
            packed = pack_rows(part[j * size : (j + 1) * size], pack)

            @pl.when(share % 2 == 0)
            def _():
                kept[share // 2, owner // SHARES] = packed

            @pl.when(share % 2 == 1)
            def _():
                sent[share // 2, owner // SHARES] = packed.astype(sent.dtype)

    for b, bank in enumerate(banks):
        first = b * depth // group
        lax.fori_loop(first, first + depth // group, functools.partial(step, bank, b * depth), None)


def bank_bytes(slabs):
    return 2 * math.prod(slabs.shape) // BANKS


def forces_call(rows_in, noise, slabs, pack):
    walkers, pairs = rows_in.shape
    n, size, _ = slabs.shape
    half = (SHARES // 2, n // SHARES, size // pack, walkers * pack)
    bank = pltpu.VMEM((n // BANKS, size, pairs), jnp.bfloat16)
    n_rest = BANKS - HELD_BANKS
    return pl.pallas_call(
        functools.partial(forces_kernel, 2, pack),
        out_shape=(
            pltpu.VMEM(half, jnp.float32),
            pltpu.VMEM(half, jnp.bfloat16),
            pltpu.VMEM((1, *half[2:]), jnp.float32),
            *[bank] * HELD_BANKS,
        ),
        in_specs=[HBM, HBM, HBM],
        out_specs=(VMEM,) * (3 + HELD_BANKS),
        scratch_shapes=[
            *[bank] * n_rest,
            pltpu.VMEM(rows_in.shape, rows_in.dtype),
            pltpu.VMEM(noise.shape, noise.dtype),
            pltpu.SemaphoreType.DMA((n + 2,)),
        ],
        compiler_params=params(MARGIN + n_rest * bank_bytes(slabs)),
        cost_estimate=pl.CostEstimate(
            flops=2 * n * size * pairs * walkers, bytes_accessed=2 * n * size * pairs, transcendentals=0
        ),
    )(*(pltpu.with_memory_space_constraint(x, pltpu.HBM) for x in (rows_in, noise, slabs)))


def split_kernel(kept, received, out, sent):
    out[...] = kept[0] + received[0].astype(jnp.float32)
    sent[...] = (kept[1] + received[1].astype(jnp.float32)).astype(sent.dtype)


def split_call(kept, received):
    return pl.pallas_call(
        split_kernel,
        out_shape=(pltpu.VMEM(kept.shape[1:], kept.dtype), pltpu.VMEM(kept.shape[1:], received.dtype)),
        in_specs=[VMEM] * 2,
        out_specs=(VMEM, VMEM),
        compiler_params=params(),
    )(kept, received)


def add_kernel(kept, received, out, sent):
    total = kept[...] + received[...].astype(jnp.float32)
    out[...] = total
    sent[...] = total.astype(sent.dtype)


def add_call(kept, received):
    return pl.pallas_call(
        add_kernel,
        out_shape=(pltpu.VMEM(kept.shape, kept.dtype), pltpu.VMEM(kept.shape, received.dtype)),
        in_specs=[VMEM] * 2,
        out_specs=(VMEM, VMEM),
        compiler_params=params(),
    )(kept, received)


def join_kernel(first, second, out):
    part = first.shape[0]
    out[:part] = first[...]
    out[part:] = second[...]


def join_call(first, second):
    return pl.pallas_call(
        join_kernel,
        out_shape=pltpu.VMEM((2 * first.shape[0], *first.shape[1:]), first.dtype),
        in_specs=[VMEM] * 2,
        out_specs=VMEM,
        compiler_params=params(),
    )(first, second)


def place_of(difference, n_high):
    place = 0
    for b in range(n_high.bit_length() - 1):
        place += ((difference >> b) & 1) * (n_high >> (b + 1))
    return place


def fields_kernel(kept, received, noise, out):
    n_high, rows, lanes = kept.shape
    me = lax.axis_index("chol")
    terms = jnp.zeros((1, lanes), jnp.float32)
    for z in range(n_high):
        capped = jnp.tanh(kept[z] + received[z].astype(jnp.float32))
        fields = noise[place_of(z ^ (me // SHARES), n_high)] - capped
        terms += jnp.sum(fields * capped - 0.5 * capped * capped, axis=0, keepdims=True)
        out[z * rows : (z + 1) * rows] = fields.astype(jnp.bfloat16)
    high = terms.astype(jnp.bfloat16).astype(jnp.float32)
    mid = (terms - high).astype(jnp.bfloat16).astype(jnp.float32)
    low = terms - high - mid
    row = lax.broadcasted_iota(jnp.int32, (TILE, lanes), 0)
    tail = jnp.where(row == 0, high, jnp.where(row == 1, mid, jnp.where(row == 2, low, 0.0)))
    out[n_high * rows :] = tail.astype(jnp.bfloat16)


def fields_call(kept, received, noise):
    n_high, rows, lanes = kept.shape
    return pl.pallas_call(
        fields_kernel,
        out_shape=jax.ShapeDtypeStruct((n_high * rows + TILE, lanes), jnp.bfloat16),
        in_specs=[VMEM] * 3,
        out_specs=VMEM,
        compiler_params=params(),
    )(kept, received, noise)


def potential_kernel(shares, pack, last, scale, *refs):
    pieces = refs[: len(shares)]
    refs = refs[len(shares) :]
    if last:
        earlier, refs = refs[:2], refs[2:]
    banks, refs = refs[:HELD_BANKS], refs[HELD_BANKS:]
    if last:
        slabs, before, out, weight, rest, sems = refs
    else:
        slabs, out, rest, sems = refs
    me = lax.axis_index("chol")
    n, size, _ = slabs.shape
    rows = size // pack
    n_high = n // SHARES
    depth = n_high // BANKS
    z_held = depth * HELD_BANKS
    spots = [share ^ lax.rem(me, SHARES) for share in shares]
    left = [(k, z) for k in range(len(shares)) for z in range(z_held, n_high)]

    def fetch(slot):
        k, z = left[slot]
        return pltpu.make_async_copy(slabs.at[z * SHARES + spots[k]], rest.at[slot], sems.at[slot])

    for slot in range(len(left)):
        fetch(slot).start()
    out[...] = before[...] if last else jnp.zeros_like(out)

    def add(piece, z, block):
        fields = unpack_rows(piece[pl.ds(pl.multiple_of(z * rows, TILE), rows)], pack)
        out[...] += lax.dot_general(
            fields, block, (((0,), (0,)), ((), ())), preferred_element_type=jnp.float32
        )

    def add_bank(b, bank, z, _):
        for spot, piece in zip(spots, pieces):
            add(piece, b * depth + z, bank[z * SHARES + spot])

    for b, bank in enumerate(banks):
        lax.fori_loop(0, depth, functools.partial(add_bank, b, bank), None)
    for slot, (k, z) in enumerate(left):
        fetch(slot).wait()
        add(pieces[k], z, rest[slot])
    if last:
        walkers = out.shape[0]
        terms = sum(
            jnp.sum(p[n_high * rows :].astype(jnp.float32), axis=0, keepdims=True)
            for p in (*pieces, *earlier)
        )
        lanes = terms.shape[1]
        whole = terms
        for i in range(1, pack):
            whole = whole + pltpu.roll(terms, i * walkers, 1)
        mine = walkers // n
        shift = lax.rem(lanes - me * mine, lanes)
        weight[...] = (pltpu.roll(jnp.broadcast_to(whole, (8, lanes)), shift, 1) * scale)[:1, :mine]


def potential_call(shares, pieces, earlier, banks, slabs, before, walkers, pack, scale):
    n, size, pairs = slabs.shape
    n_rest = n // BANKS * (BANKS - HELD_BANKS) * len(shares) // SHARES
    rest = (max(1, n_rest), size if n_rest else TILE, pairs)
    last = before is not None
    out = jax.ShapeDtypeStruct((walkers, pairs), jnp.float32)
    weight = jax.ShapeDtypeStruct((1, walkers // n), jnp.float32)
    banks = [pltpu.with_memory_space_constraint(bank, pltpu.VMEM) for bank in banks]
    slabs = pltpu.with_memory_space_constraint(slabs, pltpu.HBM)
    args = (*pieces, *earlier, *banks, slabs, before) if last else (*pieces, *banks, slabs)
    specs = [HBM if arg is slabs else VMEM for arg in args]
    work = n * size * len(shares) // SHARES
    return pl.pallas_call(
        functools.partial(potential_kernel, shares, pack, last, scale),
        out_shape=(out, weight) if last else out,
        in_specs=specs,
        out_specs=(VMEM, VMEM) if last else VMEM,
        scratch_shapes=[pltpu.VMEM(rest, jnp.bfloat16), pltpu.SemaphoreType.DMA((max(1, n_rest),))],
        compiler_params=params(MARGIN + 2 * math.prod(rest)),
        cost_estimate=pl.CostEstimate(
            flops=2 * work * pairs * walkers, bytes_accessed=2 * work * pairs, transcendentals=0
        ),
    )(*args)


def swap(block, bit, n):
    return lax.ppermute(block, "chol", [(i, i ^ bit) for i in range(n)])


def per_device(green_rows, factors, noise_draws):
    walkers = green_rows.shape[0]
    vectors, pairs = factors.shape
    n = lax.axis_size("chol")
    own = vectors // n
    pack = max(1, LANES // walkers)
    scale = 1.0 / math.sqrt(vectors)
    slabs = factors.reshape(n, own, pairs)
    high_bits = [1 << b for b in range(2, n.bit_length() - 1)]

    kept, sent, noise, *banks = forces_call(green_rows, noise_draws, slabs, pack)
    forces, sent = split_call(kept, swap(sent, 1, n))
    received = swap(sent, 2, n)
    for i, bit in enumerate(high_bits):
        noise = join_call(noise, swap(noise, high_bits[-1 - i], n))
        forces, sent = add_call(forces, received)
        received = swap(sent, bit, n)
    own_fields = fields_call(forces, received, noise)
    across = swap(own_fields, 2, n)
    beside = swap(own_fields, 1, n)
    pieces = (own_fields, beside)
    potential = potential_call((0, 1), pieces, (), banks, slabs, None, walkers, pack, scale)
    beyond = swap(across, 1, n)
    potential, weight = potential_call(
        (2, 3), (across, beyond), pieces, banks, slabs, potential, walkers, pack, scale
    )
    return (potential, weight.reshape(-1))


def solution(mesh):
    return jax.shard_map(
        per_device,
        mesh=mesh,
        in_specs=(P("groups", "chol"), P(None, "chol"), P("groups", "chol")),
        out_specs=(P("groups", "chol"), P(("groups", "chol"))),
        check_vma=False,
    )
```

```python
import functools
import math

import jax
import jax.numpy as jnp
from jax import lax
from jax.experimental import pallas as pl
from jax.experimental.pallas import tpu as pltpu
from jax.sharding import PartitionSpec as P

LANES = 128
TILE = 16
MARGIN = 4 * 1024 * 1024
SHARES = 8
BANKS = 4
COLUMNS = 1024
WIRE = jnp.float16
VMEM = pl.BlockSpec(memory_space=pltpu.VMEM)
HBM = pl.BlockSpec(memory_space=pltpu.HBM)


def params(limit=MARGIN):
    return pltpu.CompilerParams(vmem_limit_bytes=limit)


def bands_of(size):
    units = size // TILE
    ends = [-(-units * (b + 1) // BANKS) * TILE for b in range(BANKS)]
    return tuple(zip([0, *ends], ends))


def pack_rows(rows, pack):
    part = rows.shape[0] // pack
    return jnp.concatenate([rows[i * part : (i + 1) * part] for i in range(pack)], axis=1)


def unpack_rows(rows, pack):
    width = rows.shape[1] // pack
    return jnp.concatenate([rows[:, i * width : (i + 1) * width] for i in range(pack)], axis=0)


def share_of(owner, me):
    return lax.rem(owner, SHARES) ^ lax.rem(me, SHARES)


def forces_kernel(bands, pack, rows_hbm, noise_hbm, slabs, kept, sent, draws, *refs):
    *banks, rows_in, noise, sems = refs
    n, size, _ = slabs.shape
    me = lax.axis_index("chol")

    def fetch(d, b):
        lo, hi = bands[b]
        return pltpu.make_async_copy(slabs.at[d, lo:hi], banks[b].at[d], sems.at[d * BANKS + b])

    rows_copy = pltpu.make_async_copy(rows_hbm, rows_in, sems.at[n * BANKS])
    rows_copy.start()
    for d in range(n):
        for b in range(BANKS):
            fetch(d, b).start()
    noise_copy = pltpu.make_async_copy(noise_hbm, noise, sems.at[n * BANKS + 1])
    noise_copy.start()
    rows_copy.wait()

    def step(group, i, _):
        parts = []
        for j in range(group):
            for b in range(BANKS):
                fetch(i * group + j, b).wait()
        for j in range(group):
            parts += [bank[i * group + j] for bank in banks]
        part = lax.dot_general(
            jnp.concatenate(parts, axis=0),
            rows_in[...],
            (((1,), (1,)), ((), ())),
            preferred_element_type=jnp.float32,
        )
        for j in range(group):
            owner = i * group + j
            share = share_of(owner, me)
            packed = pack_rows(part[j * size : (j + 1) * size], pack)

            @pl.when(share % 2 == 0)
            def _():
                kept[share // 2, owner // SHARES] = packed

            @pl.when(share % 2 == 1)
            def _():
                sent[share // 2, owner // SHARES] = packed

    lax.fori_loop(0, n // 2 - 1, functools.partial(step, 2), None)
    lax.fori_loop(n - 2, n, functools.partial(step, 1), None)
    noise_copy.wait()
    draws[0] = pack_rows(noise[...].T, pack)


def forces_call(rows_in, noise, slabs, bands, pack):
    walkers, pairs = rows_in.shape
    n, size, _ = slabs.shape
    half = (SHARES // 2, n // SHARES, size // pack, walkers * pack)
    return pl.pallas_call(
        functools.partial(forces_kernel, bands, pack),
        out_shape=(
            pltpu.VMEM(half, jnp.float32),
            pltpu.VMEM(half, jnp.float32),
            pltpu.VMEM((1, *half[2:]), jnp.float32),
            *[pltpu.VMEM((n, hi - lo, pairs), jnp.bfloat16) for lo, hi in bands],
        ),
        in_specs=[HBM, HBM, HBM],
        out_specs=(VMEM,) * (3 + BANKS),
        scratch_shapes=[
            pltpu.VMEM(rows_in.shape, rows_in.dtype),
            pltpu.VMEM(noise.shape, noise.dtype),
            pltpu.SemaphoreType.DMA((n * BANKS + 2,)),
        ],
        compiler_params=params(),
        cost_estimate=pl.CostEstimate(
            flops=2 * n * size * pairs * walkers, bytes_accessed=2 * n * size * pairs, transcendentals=0
        ),
    )(*(pltpu.with_memory_space_constraint(x, pltpu.HBM) for x in (rows_in, noise, slabs)))


def small_call(kernel, outs, *args):
    return pl.pallas_call(
        kernel,
        out_shape=[pltpu.VMEM(shape, jnp.float32) for shape in outs],
        in_specs=[VMEM] * len(args),
        out_specs=[VMEM] * len(outs),
        compiler_params=params(),
    )(*args)


def split_kernel(kept, received, out, sent):
    for i in range(out.shape[0]):
        out[i] = kept[2 * i] + received[2 * i]
        sent[i] = kept[2 * i + 1] + received[2 * i + 1]


def add_kernel(kept, received, out):
    out[...] = kept[...] + received[...]


def join_kernel(first, second, out):
    part = first.shape[0]
    out[:part] = first[...]
    out[part:] = second[...]


def place_of(difference, n_high):
    place = 0
    for b in range(n_high.bit_length() - 1):
        place += ((difference >> b) & 1) * (n_high >> (b + 1))
    return place


def fields_kernel(kept, received, noise, out):
    n_high, rows, lanes = kept.shape
    me = lax.axis_index("chol")
    terms = jnp.zeros((1, lanes), jnp.float32)
    for z in range(n_high):
        capped = jnp.tanh(kept[z] + received[z])
        fields = noise[place_of(z ^ (me // SHARES), n_high)] - capped
        terms += jnp.sum(fields * capped - 0.5 * capped * capped, axis=0, keepdims=True)
        out[z * rows : (z + 1) * rows] = fields.astype(jnp.bfloat16)
    high = terms.astype(jnp.bfloat16).astype(jnp.float32)
    mid = (terms - high).astype(jnp.bfloat16).astype(jnp.float32)
    low = terms - high - mid
    row = lax.broadcasted_iota(jnp.int32, (TILE, lanes), 0)
    tail = jnp.where(row == 0, high, jnp.where(row == 1, mid, jnp.where(row == 2, low, 0.0)))
    out[n_high * rows :] = tail.astype(jnp.bfloat16)


def fields_call(kept, received, noise):
    n_high, rows, lanes = kept.shape
    return pl.pallas_call(
        fields_kernel,
        out_shape=pltpu.VMEM((n_high * rows + TILE, lanes), jnp.bfloat16),
        in_specs=[VMEM] * 3,
        out_specs=VMEM,
        compiler_params=params(),
    )(kept, received, noise)


def potential_kernel(shares, pack, first, last, scale, *refs):
    pieces, refs = refs[: len(shares)], refs[len(shares) :]
    if last:
        earlier, refs = refs[: SHARES - len(shares)], refs[SHARES - len(shares) :]
    banks, refs = refs[:BANKS], refs[BANKS:]
    if not first:
        before, *refs = refs
    if last:
        out, weight, total, mine, sems = refs
    else:
        (total,) = refs
    me = lax.axis_index("chol")
    n = banks[0].shape[0]
    n_high = n // SHARES
    rows = pieces[0].shape[0] // n_high // TILE * TILE
    walkers, pairs = total.shape
    width = min(COLUMNS, pairs)
    blocks = pairs // width

    def store(j):
        cols = pl.ds(j * width, width)
        return pltpu.make_async_copy(total.at[:, cols], out.at[:, cols], sems.at[j])

    weight_copy = pltpu.make_async_copy(mine, weight, sems.at[blocks]) if last else None
    if last:
        terms = sum(
            jnp.sum(p[n_high * rows :].astype(jnp.float32), axis=0, keepdims=True)
            for p in (*pieces, *earlier)
        )
        lanes = terms.shape[1]
        whole = terms
        for i in range(1, pack):
            whole = whole + pltpu.roll(terms, i * walkers, 1)
        shift = lax.rem(lanes - me * (walkers // n), lanes)
        rolled = pltpu.roll(jnp.broadcast_to(whole, (8, lanes)), shift, 1) * scale
        mine[...] = rolled[:1, : walkers // n]
        weight_copy.start()
    fields, places = [], []
    for share, piece in zip(shares, pieces):
        for z in range(n_high):
            fields.append(unpack_rows(piece[z * rows : (z + 1) * rows], pack))
            places.append(z * SHARES + (share ^ lax.rem(me, SHARES)))
    columns = jnp.concatenate(fields, axis=0)
    for j in range(blocks):
        cols = slice(j * width, (j + 1) * width)
        block = jnp.concatenate([bank[at, :, cols] for at in places for bank in banks], axis=0)
        part = lax.dot_general(
            columns, block, (((0,), (0,)), ((), ())), preferred_element_type=jnp.float32
        )
        total[:, cols] = part if first else before[:, cols] + part
        if last:
            store(j).start()
    if last:
        weight_copy.wait()
        for j in range(blocks):
            store(j).wait()


def potential_call(shares, pieces, earlier, banks, before, walkers, pack, scale):
    n, _, pairs = banks[0].shape
    first, last = before is None, bool(earlier)
    total = pltpu.VMEM((walkers, pairs), jnp.float32)
    mine = pltpu.VMEM((1, walkers // n), jnp.float32)
    out = jax.ShapeDtypeStruct(total.shape, jnp.float32)
    weight = jax.ShapeDtypeStruct(mine.shape, jnp.float32)
    work = sum(bank.shape[0] * bank.shape[1] for bank in banks) * len(shares) // SHARES
    banks = [pltpu.with_memory_space_constraint(bank, pltpu.VMEM) for bank in banks]
    args = [*pieces, *earlier, *banks, *([] if first else [before])]
    blocks = pairs // min(COLUMNS, pairs)
    return pl.pallas_call(
        functools.partial(potential_kernel, shares, pack, first, last, scale),
        out_shape=(out, weight) if last else total,
        in_specs=[VMEM] * len(args),
        out_specs=(HBM, HBM) if last else VMEM,
        scratch_shapes=[total, mine, pltpu.SemaphoreType.DMA((blocks + 1,))] if last else [],
        compiler_params=params(),
        cost_estimate=pl.CostEstimate(
            flops=2 * work * pairs * walkers, bytes_accessed=2 * work * pairs, transcendentals=0
        ),
    )(*args)


def swap(block, bit, n):
    return lax.ppermute(block, "chol", [(i, i ^ bit) for i in range(n)])


def send(block, bit, n):
    return swap(block.astype(WIRE), bit, n).astype(jnp.float32)


ROUNDS = ((0,), (1, 4, 2), (5, 3, 6), (7,))


def per_device(green_rows, factors, noise_draws):
    walkers = green_rows.shape[0]
    vectors, pairs = factors.shape
    n = lax.axis_size("chol")
    own = vectors // n
    pack = max(1, LANES // walkers)
    scale = 1.0 / math.sqrt(vectors)
    slabs = factors.reshape(n, own, pairs)
    bands = bands_of(own)
    low_bits = [1 << b for b in range(SHARES.bit_length() - 1)]
    high_bits = [1 << b for b in range(SHARES.bit_length() - 1, n.bit_length() - 1)]

    forces, sent, noise, *banks = forces_call(green_rows, noise_draws, slabs, bands, pack)
    received = send(sent, low_bits[0], n)
    for bit in low_bits[1:]:
        part = (forces.shape[0] // 2, *forces.shape[1:])
        forces, sent = small_call(split_kernel, [part, part], forces, received)
        received = send(sent, bit, n)
    forces, received = forces[0], received[0]
    for i, bit in enumerate(high_bits):
        other = swap(noise, high_bits[-1 - i], n)
        (noise,) = small_call(join_kernel, [(2 * noise.shape[0], *noise.shape[1:])], noise, other)
        (forces,) = small_call(add_kernel, [forces.shape], forces, received)
        received = send(forces, bit, n)

    pieces = {0: fields_call(forces, received, noise)}
    for share, source, bit in ((4, 0, 4), (2, 0, 2), (1, 0, 1), (6, 4, 2), (5, 4, 1), (3, 2, 1), (7, 6, 1)):
        pieces[share] = swap(pieces[source], bit, n)
    potential, used = None, ()
    for i, shares in enumerate(ROUNDS):
        here = tuple(pieces[share] for share in shares)
        earlier = used if i == len(ROUNDS) - 1 else ()
        potential = potential_call(shares, here, earlier, banks, potential, walkers, pack, scale)
        used += here
    potential, weight = potential
    return (potential, weight.reshape(-1))


def solution(mesh):
    return jax.shard_map(
        per_device,
        mesh=mesh,
        in_specs=(P("groups", "chol"), P(None, "chol"), P("groups", "chol")),
        out_specs=(P("groups", "chol"), P(("groups", "chol"))),
        check_vma=False,
    )
```

```python
import functools
import math

import jax
import jax.numpy as jnp
from jax import lax
from jax.experimental import pallas as pl
from jax.experimental.pallas import tpu as pltpu
from jax.sharding import PartitionSpec as P

LANES = 128
TILE = 16
MARGIN = 4 * 1024 * 1024
PRODUCT_LIMIT = 10 * 1024 * 1024
SHARES = 8
BANKS = 4
COLUMNS = 1024
WIRE = jnp.float16
VMEM = pl.BlockSpec(memory_space=pltpu.VMEM)
HBM = pl.BlockSpec(memory_space=pltpu.HBM)


def params(limit=MARGIN):
    return pltpu.CompilerParams(vmem_limit_bytes=limit)


def bands_of(size):
    units = size // TILE
    ends = [-(-units * (b + 1) // BANKS) * TILE for b in range(BANKS)]
    return tuple(zip([0, *ends], ends))


def pack_rows(rows, pack):
    part = rows.shape[0] // pack
    return jnp.concatenate([rows[i * part : (i + 1) * part] for i in range(pack)], axis=1)


def unpack_rows(rows, pack):
    width = rows.shape[1] // pack
    return jnp.concatenate([rows[:, i * width : (i + 1) * width] for i in range(pack)], axis=0)


def share_of(owner, me):
    return lax.rem(owner, SHARES) ^ lax.rem(me, SHARES)


def forces_kernel(bands, pack, rows_hbm, noise_hbm, slabs, halves, draws, *refs):
    *banks, rows_in, noise, sems = refs
    n, _, _ = slabs.shape
    me = lax.axis_index("chol")

    def fetch(d, b):
        lo, hi = bands[b]
        return pltpu.make_async_copy(slabs.at[d, lo:hi], banks[b].at[d], sems.at[d * BANKS + b])

    noise_copy = pltpu.make_async_copy(noise_hbm, noise, sems.at[n * BANKS + 1])
    noise_copy.start()
    rows_copy = pltpu.make_async_copy(rows_hbm, rows_in, sems.at[n * BANKS])
    rows_copy.start()
    for d in range(n):
        for b in range(BANKS):
            fetch(d, b).start()
    noise_copy.wait()
    draws[0] = pack_rows(noise[...].T, pack)
    rows_copy.wait()

    def step(group, i, _):
        for j in range(group):
            for b in range(BANKS):
                fetch(i * group + j, b).wait()
        for j in range(group):
            owner = i * group + j
            part = lax.dot_general(
                jnp.concatenate([bank[owner] for bank in banks], axis=0),
                rows_in[...],
                (((1,), (1,)), ((), ())),
                preferred_element_type=jnp.float32,
            )
            share = share_of(owner, me)
            halves[share % 2, share // 2, owner // SHARES] = pack_rows(part, pack)

    lax.fori_loop(0, n // 2, functools.partial(step, 2), None)


def forces_call(rows_in, noise, slabs, bands, pack):
    walkers, pairs = rows_in.shape
    n, size, _ = slabs.shape
    halves = (2, SHARES // 2, n // SHARES, size // pack, walkers * pack)
    return pl.pallas_call(
        functools.partial(forces_kernel, bands, pack),
        out_shape=(
            pltpu.VMEM(halves, jnp.float32),
            pltpu.VMEM((1, *halves[3:]), jnp.float32),
            *[pltpu.VMEM((n, hi - lo, pairs), jnp.bfloat16) for lo, hi in bands],
        ),
        in_specs=[HBM, HBM, HBM],
        out_specs=(VMEM,) * (2 + BANKS),
        scratch_shapes=[
            pltpu.VMEM(rows_in.shape, rows_in.dtype),
            pltpu.VMEM(noise.shape, noise.dtype),
            pltpu.SemaphoreType.DMA((n * BANKS + 2,)),
        ],
        compiler_params=params(),
        cost_estimate=pl.CostEstimate(
            flops=2 * n * size * pairs * walkers, bytes_accessed=2 * n * size * pairs, transcendentals=0
        ),
    )(*(pltpu.with_memory_space_constraint(x, pltpu.HBM) for x in (rows_in, noise, slabs)))


def small_call(kernel, outs, *args):
    return pl.pallas_call(
        kernel,
        out_shape=[pltpu.VMEM(shape, jnp.float32) for shape in outs],
        in_specs=[VMEM] * len(args),
        out_specs=[VMEM] * len(outs),
        compiler_params=params(),
    )(*args)


def spread_kernel(halves, received, *outs):
    for k, out in enumerate(outs):
        out[...] = halves[0, k] + received[k]


def sum_kernel(kept, *refs):
    *received, out = refs
    total = kept[...]
    for ref in received:
        total += ref[...]
    out[...] = total


def add_kernel(kept, received, out):
    out[...] = kept[...] + received[...]


def join_kernel(first, second, out):
    part = first.shape[0]
    out[:part] = first[...]
    out[part:] = second[...]


def place_of(difference, n_high):
    place = 0
    for b in range(n_high.bit_length() - 1):
        place += ((difference >> b) & 1) * (n_high >> (b + 1))
    return place


def fields_kernel(kept, received, noise, out):
    n_high, rows, lanes = kept.shape
    me = lax.axis_index("chol")
    terms = jnp.zeros((1, lanes), jnp.float32)
    for z in range(n_high):
        capped = jnp.tanh(kept[z] + received[z])
        fields = noise[place_of(z ^ (me // SHARES), n_high)] - capped
        terms += jnp.sum(fields * capped - 0.5 * capped * capped, axis=0, keepdims=True)
        out[z * rows : (z + 1) * rows] = fields.astype(jnp.bfloat16)
    high = terms.astype(jnp.bfloat16).astype(jnp.float32)
    mid = (terms - high).astype(jnp.bfloat16).astype(jnp.float32)
    low = terms - high - mid
    row = lax.broadcasted_iota(jnp.int32, (TILE, lanes), 0)
    tail = jnp.where(row == 0, high, jnp.where(row == 1, mid, jnp.where(row == 2, low, 0.0)))
    out[n_high * rows :] = tail.astype(jnp.bfloat16)


def fields_call(kept, received, noise):
    n_high, rows, lanes = kept.shape
    return pl.pallas_call(
        fields_kernel,
        out_shape=pltpu.VMEM((n_high * rows + TILE, lanes), jnp.bfloat16),
        in_specs=[VMEM] * 3,
        out_specs=VMEM,
        compiler_params=params(),
    )(kept, received, noise)


def potential_kernel(shares, pack, first, last, scale, *refs):
    pieces, refs = refs[: len(shares)], refs[len(shares) :]
    if last:
        earlier, refs = refs[: SHARES - len(shares)], refs[SHARES - len(shares) :]
    banks, refs = refs[:BANKS], refs[BANKS:]
    if not first:
        before, *refs = refs
    if last:
        out, weight, total, mine, sems = refs
    else:
        (total,) = refs
    me = lax.axis_index("chol")
    n = banks[0].shape[0]
    n_high = n // SHARES
    rows = pieces[0].shape[0] // n_high // TILE * TILE
    walkers, pairs = total.shape
    width = min(COLUMNS, pairs)
    blocks = pairs // width

    def store(j):
        cols = pl.ds(j * width, width)
        return pltpu.make_async_copy(total.at[:, cols], out.at[:, cols], sems.at[j])

    weight_copy = pltpu.make_async_copy(mine, weight, sems.at[blocks]) if last else None
    if last:
        terms = sum(
            jnp.sum(p[n_high * rows :].astype(jnp.float32), axis=0, keepdims=True)
            for p in (*pieces, *earlier)
        )
        lanes = terms.shape[1]
        whole = terms
        for i in range(1, pack):
            whole = whole + pltpu.roll(terms, i * walkers, 1)
        shift = lax.rem(lanes - me * (walkers // n), lanes)
        rolled = pltpu.roll(jnp.broadcast_to(whole, (8, lanes)), shift, 1) * scale
        mine[...] = rolled[:1, : walkers // n]
        weight_copy.start()
    fields, places = [], []
    for share, piece in zip(shares, pieces):
        for z in range(n_high):
            fields.append(unpack_rows(piece[z * rows : (z + 1) * rows], pack))
            places.append(z * SHARES + (share ^ lax.rem(me, SHARES)))
    columns = jnp.concatenate(fields, axis=0)
    for j in range(blocks):
        cols = slice(j * width, (j + 1) * width)
        block = jnp.concatenate([bank[at, :, cols] for at in places for bank in banks], axis=0)
        part = lax.dot_general(
            columns, block, (((0,), (0,)), ((), ())), preferred_element_type=jnp.float32
        )
        total[:, cols] = part if first else before[:, cols] + part
        if last:
            store(j).start()
    if last:
        weight_copy.wait()
        for j in range(blocks):
            store(j).wait()


def potential_call(shares, pieces, earlier, banks, before, walkers, pack, scale):
    n, _, pairs = banks[0].shape
    first, last = before is None, bool(earlier)
    total = pltpu.VMEM((walkers, pairs), jnp.float32)
    mine = pltpu.VMEM((1, walkers // n), jnp.float32)
    out = jax.ShapeDtypeStruct(total.shape, jnp.float32)
    weight = jax.ShapeDtypeStruct(mine.shape, jnp.float32)
    work = sum(bank.shape[0] * bank.shape[1] for bank in banks) * len(shares) // SHARES
    banks = [pltpu.with_memory_space_constraint(bank, pltpu.VMEM) for bank in banks]
    args = [*pieces, *earlier, *banks, *([] if first else [before])]
    blocks = pairs // min(COLUMNS, pairs)
    return pl.pallas_call(
        functools.partial(potential_kernel, shares, pack, first, last, scale),
        out_shape=(out, weight) if last else total,
        in_specs=[VMEM] * len(args),
        out_specs=(HBM, HBM) if last else VMEM,
        scratch_shapes=[total, mine, pltpu.SemaphoreType.DMA((blocks + 1,))] if last else [],
        compiler_params=params(PRODUCT_LIMIT),
        cost_estimate=pl.CostEstimate(
            flops=2 * work * pairs * walkers, bytes_accessed=2 * work * pairs, transcendentals=0
        ),
    )(*args)


def swap(block, bit, n):
    return lax.ppermute(block, "chol", [(i, i ^ bit) for i in range(n)])


def send(block, bit, n):
    return swap(block.astype(WIRE), bit, n).astype(jnp.float32)


ROUNDS = ((0, 1), (4, 2, 5, 3), (6,), (7,))


def per_device(green_rows, factors, noise_draws):
    walkers = green_rows.shape[0]
    vectors, pairs = factors.shape
    n = lax.axis_size("chol")
    own = vectors // n
    pack = max(1, LANES // walkers)
    scale = 1.0 / math.sqrt(vectors)
    slabs = factors.reshape(n, own, pairs)
    bands = bands_of(own)
    high_bits = [1 << b for b in range(SHARES.bit_length() - 1, n.bit_length() - 1)]

    halves, noise, *banks = forces_call(green_rows, noise_draws, slabs, bands, pack)
    received = send(halves[1], 1, n)
    part = halves.shape[2:]
    forces, *sent = small_call(spread_kernel, [part] * (SHARES // 2), halves, received)
    arrived = [send(block, 2 * k + 2, n) for k, block in enumerate(sent)]
    (forces,) = small_call(sum_kernel, [part], forces, *arrived)
    received = None
    for i, bit in enumerate(high_bits):
        other = swap(noise, high_bits[-1 - i], n)
        (noise,) = small_call(join_kernel, [(2 * noise.shape[0], *noise.shape[1:])], noise, other)
        if received is not None:
            (forces,) = small_call(add_kernel, [part], forces, received)
        received = send(forces, bit, n)

    pieces = {0: fields_call(forces, received, noise)}
    for share, source, bit in ((4, 0, 4), (2, 0, 2), (1, 0, 1), (6, 4, 2), (5, 4, 1), (3, 2, 1), (7, 6, 1)):
        pieces[share] = swap(pieces[source], bit, n)
    potential, used = None, ()
    for i, shares in enumerate(ROUNDS):
        here = tuple(pieces[share] for share in shares)
        earlier = used if i == len(ROUNDS) - 1 else ()
        potential = potential_call(shares, here, earlier, banks, potential, walkers, pack, scale)
        used += here
    potential, weight = potential
    return (potential, weight.reshape(-1))


def solution(mesh):
    return jax.shard_map(
        per_device,
        mesh=mesh,
        in_specs=(P("groups", "chol"), P(None, "chol"), P("groups", "chol")),
        out_specs=(P("groups", "chol"), P(("groups", "chol"))),
        check_vma=False,
    )
```

```python
import functools
import math

import jax
import jax.numpy as jnp
from jax import lax
from jax.experimental import pallas as pl
from jax.experimental.pallas import tpu as pltpu
from jax.sharding import PartitionSpec as P

LANES = 128
TILE = 16
MARGIN = 4 * 1024 * 1024
PRODUCT_LIMIT = 10 * 1024 * 1024
SHARES = 8
BANKS = 4
COLUMNS = 512
WIRE = jnp.float16
VMEM = pl.BlockSpec(memory_space=pltpu.VMEM)
HBM = pl.BlockSpec(memory_space=pltpu.HBM)


def params(limit=MARGIN):
    return pltpu.CompilerParams(vmem_limit_bytes=limit)


def bands_of(size):
    units = size // TILE
    ends = [-(-units * (b + 1) // BANKS) * TILE for b in range(BANKS)]
    return tuple(zip([0, *ends], ends))


def pack_rows(rows, pack):
    part = rows.shape[0] // pack
    return jnp.concatenate([rows[i * part : (i + 1) * part] for i in range(pack)], axis=1)


def unpack_rows(rows, pack):
    width = rows.shape[1] // pack
    return jnp.concatenate([rows[:, i * width : (i + 1) * width] for i in range(pack)], axis=0)


def share_of(owner, me):
    return lax.rem(owner, SHARES) ^ lax.rem(me, SHARES)


def forces_kernel(bands, pack, rows_hbm, noise_hbm, slabs, halves, draws, *refs):
    *banks, rows_in, noise, sems = refs
    n, _, _ = slabs.shape
    me = lax.axis_index("chol")

    def fetch(d, b):
        lo, hi = bands[b]
        return pltpu.make_async_copy(slabs.at[d, lo:hi], banks[b].at[d], sems.at[d * BANKS + b])

    noise_copy = pltpu.make_async_copy(noise_hbm, noise, sems.at[n * BANKS + 1])
    noise_copy.start()
    rows_copy = pltpu.make_async_copy(rows_hbm, rows_in, sems.at[n * BANKS])
    rows_copy.start()
    for d in range(n):
        for b in range(BANKS):
            fetch(d, b).start()
    noise_copy.wait()
    draws[0] = pack_rows(noise[...].T, pack)
    rows_copy.wait()

    def step(group, i, _):
        for j in range(group):
            for b in range(BANKS):
                fetch(i * group + j, b).wait()
        for j in range(group):
            owner = i * group + j
            part = lax.dot_general(
                jnp.concatenate([bank[owner] for bank in banks], axis=0),
                rows_in[...],
                (((1,), (1,)), ((), ())),
                preferred_element_type=jnp.float32,
            )
            share = share_of(owner, me)
            halves[share % 2, share // 2, owner // SHARES] = pack_rows(part, pack)

    lax.fori_loop(0, n // 2, functools.partial(step, 2), None)


def forces_call(rows_in, noise, slabs, bands, pack):
    walkers, pairs = rows_in.shape
    n, size, _ = slabs.shape
    halves = (2, SHARES // 2, n // SHARES, size // pack, walkers * pack)
    return pl.pallas_call(
        functools.partial(forces_kernel, bands, pack),
        out_shape=(
            pltpu.VMEM(halves, jnp.float32),
            pltpu.VMEM((1, *halves[3:]), jnp.float32),
            *[pltpu.VMEM((n, hi - lo, pairs), jnp.bfloat16) for lo, hi in bands],
        ),
        in_specs=[HBM, HBM, HBM],
        out_specs=(VMEM,) * (2 + BANKS),
        scratch_shapes=[
            pltpu.VMEM(rows_in.shape, rows_in.dtype),
            pltpu.VMEM(noise.shape, noise.dtype),
            pltpu.SemaphoreType.DMA((n * BANKS + 2,)),
        ],
        compiler_params=params(),
        cost_estimate=pl.CostEstimate(
            flops=2 * n * size * pairs * walkers, bytes_accessed=2 * n * size * pairs, transcendentals=0
        ),
    )(*(pltpu.with_memory_space_constraint(x, pltpu.HBM) for x in (rows_in, noise, slabs)))


def small_call(kernel, outs, *args):
    return pl.pallas_call(
        kernel,
        out_shape=[pltpu.VMEM(shape, jnp.float32) for shape in outs],
        in_specs=[VMEM] * len(args),
        out_specs=[VMEM] * len(outs),
        compiler_params=params(),
    )(*args)


def sum_kernel(kept, *refs):
    *received, out = refs
    total = kept[...]
    for ref in received:
        total += ref[...]
    out[...] = total


def add_kernel(kept, received, out):
    out[...] = kept[...] + received[...]


def join_kernel(first, second, out):
    part = first.shape[0]
    out[:part] = first[...]
    out[part:] = second[...]


def place_of(difference, n_high):
    place = 0
    for b in range(n_high.bit_length() - 1):
        place += ((difference >> b) & 1) * (n_high >> (b + 1))
    return place


def fields_kernel(kept, received, noise, out):
    n_high, rows, lanes = kept.shape
    me = lax.axis_index("chol")
    terms = jnp.zeros((1, lanes), jnp.float32)
    for z in range(n_high):
        capped = jnp.tanh(kept[z] + received[z])
        fields = noise[place_of(z ^ (me // SHARES), n_high)] - capped
        terms += jnp.sum(fields * capped - 0.5 * capped * capped, axis=0, keepdims=True)
        out[z * rows : (z + 1) * rows] = fields.astype(jnp.bfloat16)
    high = terms.astype(jnp.bfloat16).astype(jnp.float32)
    mid = (terms - high).astype(jnp.bfloat16).astype(jnp.float32)
    low = terms - high - mid
    row = lax.broadcasted_iota(jnp.int32, (TILE, lanes), 0)
    tail = jnp.where(row == 0, high, jnp.where(row == 1, mid, jnp.where(row == 2, low, 0.0)))
    out[n_high * rows :] = tail.astype(jnp.bfloat16)


def fields_call(kept, received, noise):
    n_high, rows, lanes = kept.shape
    return pl.pallas_call(
        fields_kernel,
        out_shape=pltpu.VMEM((n_high * rows + TILE, lanes), jnp.bfloat16),
        in_specs=[VMEM] * 3,
        out_specs=VMEM,
        compiler_params=params(),
    )(kept, received, noise)


def potential_kernel(shares, pack, first, last, scale, *refs):
    pieces, refs = refs[: len(shares)], refs[len(shares) :]
    if last:
        earlier, refs = refs[: SHARES - len(shares)], refs[SHARES - len(shares) :]
    banks, refs = refs[:BANKS], refs[BANKS:]
    if not first:
        before, *refs = refs
    if last:
        out, weight, total, mine, sems = refs
    else:
        (total,) = refs
    me = lax.axis_index("chol")
    n = banks[0].shape[0]
    n_high = n // SHARES
    rows = pieces[0].shape[0] // n_high // TILE * TILE
    walkers, pairs = total.shape
    width = min(COLUMNS, pairs)
    blocks = pairs // width

    def store(j):
        cols = pl.ds(j * width, width)
        return pltpu.make_async_copy(total.at[:, cols], out.at[:, cols], sems.at[j])

    weight_copy = pltpu.make_async_copy(mine, weight, sems.at[blocks]) if last else None
    if last:
        terms = sum(
            jnp.sum(p[n_high * rows :].astype(jnp.float32), axis=0, keepdims=True)
            for p in (*pieces, *earlier)
        )
        lanes = terms.shape[1]
        whole = terms
        for i in range(1, pack):
            whole = whole + pltpu.roll(terms, i * walkers, 1)
        shift = lax.rem(lanes - me * (walkers // n), lanes)
        rolled = pltpu.roll(jnp.broadcast_to(whole, (8, lanes)), shift, 1) * scale
        mine[...] = rolled[:1, : walkers // n]
        weight_copy.start()
    fields, places = [], []
    for share, piece in zip(shares, pieces):
        for z in range(n_high):
            fields.append(unpack_rows(piece[z * rows : (z + 1) * rows], pack))
            places.append(z * SHARES + (share ^ lax.rem(me, SHARES)))
    columns = jnp.concatenate(fields, axis=0)
    for j in range(blocks):
        cols = slice(j * width, (j + 1) * width)
        block = jnp.concatenate([bank[at, :, cols] for at in places for bank in banks], axis=0)
        part = lax.dot_general(
            columns, block, (((0,), (0,)), ((), ())), preferred_element_type=jnp.float32
        )
        total[:, cols] = part if first else before[:, cols] + part
        if last:
            store(j).start()
    if last:
        weight_copy.wait()
        for j in range(blocks):
            store(j).wait()


def potential_call(shares, pieces, earlier, banks, before, walkers, pack, scale):
    n, _, pairs = banks[0].shape
    first, last = before is None, bool(earlier)
    total = pltpu.VMEM((walkers, pairs), jnp.float32)
    mine = pltpu.VMEM((1, walkers // n), jnp.float32)
    out = jax.ShapeDtypeStruct(total.shape, jnp.float32)
    weight = jax.ShapeDtypeStruct(mine.shape, jnp.float32)
    work = sum(bank.shape[0] * bank.shape[1] for bank in banks) * len(shares) // SHARES
    banks = [pltpu.with_memory_space_constraint(bank, pltpu.VMEM) for bank in banks]
    args = [*pieces, *earlier, *banks, *([] if first else [before])]
    blocks = pairs // min(COLUMNS, pairs)
    return pl.pallas_call(
        functools.partial(potential_kernel, shares, pack, first, last, scale),
        out_shape=(out, weight) if last else total,
        in_specs=[VMEM] * len(args),
        out_specs=(HBM, HBM) if last else VMEM,
        scratch_shapes=[total, mine, pltpu.SemaphoreType.DMA((blocks + 1,))] if last else [],
        compiler_params=params(PRODUCT_LIMIT),
        cost_estimate=pl.CostEstimate(
            flops=2 * work * pairs * walkers, bytes_accessed=2 * work * pairs, transcendentals=0
        ),
    )(*args)


def swap(block, bit, n):
    return lax.ppermute(block, "chol", [(i, i ^ bit) for i in range(n)])


def send(block, bit, n):
    return swap(block.astype(WIRE), bit, n).astype(jnp.float32)


ROUNDS = ((0, 1), (4, 2, 5, 3), (6,), (7,))


def per_device(green_rows, factors, noise_draws):
    walkers = green_rows.shape[0]
    vectors, pairs = factors.shape
    n = lax.axis_size("chol")
    own = vectors // n
    pack = max(1, LANES // walkers)
    scale = 1.0 / math.sqrt(vectors)
    slabs = factors.reshape(n, own, pairs)
    bands = bands_of(own)
    high_bits = [1 << b for b in range(SHARES.bit_length() - 1, n.bit_length() - 1)]

    halves, noise, *banks = forces_call(green_rows, noise_draws, slabs, bands, pack)
    received = send(halves[1], 1, n)
    part = halves.shape[2:]
    forces, *sent = [halves[0, k] + received[k] for k in range(SHARES // 2)]
    arrived = [send(block, 2 * k + 2, n) for k, block in enumerate(sent)]
    (forces,) = small_call(sum_kernel, [part], forces, *arrived)
    received = None
    for i, bit in enumerate(high_bits):
        other = swap(noise, high_bits[-1 - i], n)
        (noise,) = small_call(join_kernel, [(2 * noise.shape[0], *noise.shape[1:])], noise, other)
        if received is not None:
            (forces,) = small_call(add_kernel, [part], forces, received)
        received = send(forces, bit, n)

    pieces = {0: fields_call(forces, received, noise)}
    for share, source, bit in ((4, 0, 4), (2, 0, 2), (1, 0, 1), (6, 4, 2), (5, 4, 1), (3, 2, 1), (7, 6, 1)):
        pieces[share] = swap(pieces[source], bit, n)
    potential, used = None, ()
    for i, shares in enumerate(ROUNDS):
        here = tuple(pieces[share] for share in shares)
        earlier = used if i == len(ROUNDS) - 1 else ()
        potential = potential_call(shares, here, earlier, banks, potential, walkers, pack, scale)
        used += here
    potential, weight = potential
    return (potential, weight.reshape(-1))


def solution(mesh):
    return jax.shard_map(
        per_device,
        mesh=mesh,
        in_specs=(P("groups", "chol"), P(None, "chol"), P("groups", "chol")),
        out_specs=(P("groups", "chol"), P(("groups", "chol"))),
        check_vma=False,
    )
```
